32 devices in a mesh: groups: 2 (over x), tensor: 8 (over z, y), dp: 2 (over core).
Axes of the slice: x: 2, y: 2, z: 4, core: 2. Of those that a mesh axis runs over, the one named last changes fastest.
Arguments:
- inputs: bfloat16 [4, 256, 16384], P(('groups', 'dp'), None, 'tensor'), parts along dimension 0, may hold values from -6 to 6
- cross_w: bfloat16 [16384, 16384], P('dp', 'tensor'), may hold values from -0.046875 to 0.046875
- cross_b: float32 [16384], P('tensor'), may hold values from -3 to 3
- mix_weight: bfloat16 [128, 512], replicated, may hold values from -0.5 to 0.5
- mix_bias: float32 [512], replicated, may hold values from -3 to 3
- out_weight: bfloat16 [512, 128], replicated, may hold values from -0.25 to 0.25
- cotangent: bfloat16 [4, 256, 16384], P(('groups', 'dp'), 'tensor'), parts along dimension 0, may hold values from -12 to 12
Outputs:
- compressed: bfloat16 [4, 256, 16384], P(('groups', 'dp'), 'tensor'), parts along dimension 0
- grad_inputs: bfloat16 [4, 256, 16384], P(('groups', 'dp'), None, 'tensor'), parts along dimension 0
- grad_mix: float32 [256, 512], P('groups'), parts along dimension 0
- grad_mix_bias: float32 [1024], P('groups'), parts along dimension 0
- grad_out: float32 [1024, 128], P('groups'), parts along dimension 0
The draws below stay inside these ranges and needn't reach their ends.
There are 2 independent parts, one for each index of `groups`. The reference program is written for one: setup_inputs(seed, part) draws one part's arguments, and reference() takes and returns one part's arrays. A program takes and returns all parts, laid end to end along the dimension named above; an argument that names none is the same for every part. Nothing has to cross between parts.
All inputs are finite; a program needn't handle non-finite values.
Results may differ from the reference program's by a relative error of at most 0.019.
Values may be sent and summed in bfloat16 or wider, within the bound.
No kernel may reach another device: no remote copies, remote signals or barrier semaphores. Data moves between devices by JAX's collectives and lax.ppermute only.
A program may use at most 256 MiB of HBM per device.

```python
import jax
import jax.numpy as jnp
from jax import lax

F = 128
E = 128
H = 512
K = 128
ROWS = 256
D = 16384
N_TENSOR = 8
N_DP = 2


def level_of(key, extent, cuts, least, top_value):
    factor_of, own = 1.0, jax.random.fold_in(key, 6)
    for axis_at, parts in cuts:
        steps = jnp.exp(jax.random.uniform(jax.random.fold_in(own, axis_at), (parts,), jnp.float32, least / len(cuts), top_value / len(cuts)))
        factor_of = factor_of * jnp.repeat(steps, extent[axis_at] // parts).reshape([-1 if axis == axis_at else 1 for axis in range(len(extent))])
    return factor_of


def gaussian(own_key, shape, deviation, bound, shards=(), held_as=jnp.bfloat16):
    values = jax.random.normal(own_key, shape, jnp.float32) * deviation
    if len(shards) > 0:
        values = level_of(own_key, shape, shards, -0.22, 0.18) * values
    return jnp.clip(values, min=-bound, max=bound).astype(held_as)


def setup_inputs(seed: int = 0, part: int = 0) -> dict:
    key_of = jax.random.split(jax.random.key(seed), 8)
    own_keys = jax.random.split(jax.random.fold_in(key_of[7], part), 8)
    inputs = gaussian(own_keys[0], (N_DP, ROWS, D), 1.0, 6.0, ((0, 2), (2, 8)))
    cross_w = gaussian(key_of[1], (D, D), D ** -0.5, 0.046875, ((0, 2), (1, 8)))
    cross_b = gaussian(key_of[2], (D,), 0.5, 3.0, ((0, 8),), jnp.float32)
    mix_weight = gaussian(key_of[3], (F, H), F ** -0.5, 0.5)
    mix_bias = gaussian(key_of[4], (H,), 0.5, 3.0, (), jnp.float32)
    out_weight = gaussian(key_of[5], (H, K), H ** -0.5, 0.25)
    cotangent = gaussian(own_keys[6], (N_DP, ROWS, F * K), 2.0, 12.0, ((0, 2), (1, 8)))
    return dict(inputs=inputs, cross_w=cross_w, cross_b=cross_b, mix_weight=mix_weight, mix_bias=mix_bias, out_weight=out_weight, cotangent=cotangent)


def reference(inputs, cross_w, cross_b, mix_weight, mix_bias, out_weight, cotangent):
    row_total = N_DP * ROWS
    flat_rows = inputs.reshape(row_total, D)
    linear = jnp.dot(flat_rows, cross_w, preferred_element_type=jnp.float32) + cross_b
    base_rows = flat_rows.astype(jnp.float32)
    crossed = (base_rows * linear + base_rows).astype(jnp.bfloat16)
    feature_grid = crossed.reshape(row_total, F, E).astype(jnp.float32)
    gram_rows = (jnp.einsum("bfe,bge->bfg", feature_grid, feature_grid) / E).astype(jnp.bfloat16)
    gram_wide = gram_rows.astype(jnp.float32)
    pre_act = jnp.einsum("bfg,gh->bfh", gram_wide, mix_weight.astype(jnp.float32)) + mix_bias
    sigmoid_pre = jax.nn.sigmoid(pre_act)
    hidden = (pre_act * sigmoid_pre).astype(jnp.bfloat16)
    hidden_wide = hidden.astype(jnp.float32)
    compressed = jnp.einsum("bfh,hk->bfk", hidden_wide, out_weight.astype(jnp.float32)).astype(jnp.bfloat16)
    upstream = cotangent.reshape(row_total, F, K).astype(jnp.float32)
    d_hidden = jnp.einsum("bfk,hk->bfh", upstream, out_weight.astype(jnp.float32))
    grad_out = jnp.einsum("bfh,bfk->hk", hidden_wide, upstream) / row_total
    d_pre = (d_hidden * sigmoid_pre * (1.0 + pre_act * (1.0 - sigmoid_pre))).astype(jnp.bfloat16)
    d_pre_wide = d_pre.astype(jnp.float32)
    grad_mix = jnp.einsum("bfg,bfh->gh", gram_wide, d_pre_wide) / row_total
    grad_mix_bias = jnp.sum(d_pre_wide, axis=(0, 1)) / row_total
    d_gram = jnp.einsum("bfh,gh->bfg", d_pre_wide, mix_weight.astype(jnp.float32))
    d_grid = jnp.einsum("bfg,bge->bfe", d_gram + jnp.swapaxes(d_gram, 1, 2), feature_grid) / E
    d_crossed = d_grid.astype(jnp.bfloat16).reshape(row_total, D)
    d_crossed_wide = d_crossed.astype(jnp.float32)
    d_linear = (d_crossed_wide * base_rows).astype(jnp.bfloat16)
    block_width = D // N_TENSOR

    def add_block(running, block_index):
        offset = (block_index * block_width).astype(jnp.int32)
        grad_block = lax.dynamic_slice_in_dim(d_linear, offset, block_width, 1)
        weight_block = lax.dynamic_slice_in_dim(cross_w, offset, block_width, 1)
        block_term = lax.dot_general(grad_block, weight_block, (((1,), (1,)), ((), ())), preferred_element_type=jnp.float32)
        rounded = lax.optimization_barrier(block_term.astype(jnp.bfloat16))
        return running + rounded.astype(jnp.float32), None

    back_sum, _ = lax.scan(add_block, jnp.zeros((row_total, D), jnp.float32), jnp.arange(N_TENSOR, dtype=jnp.int32))
    grad_inputs = (d_crossed_wide * (linear + 1.0) + back_sum).astype(jnp.bfloat16)
    return (compressed.reshape(N_DP, ROWS, F * K), grad_inputs.reshape(N_DP, ROWS, D), grad_mix, grad_mix_bias, grad_out)
```

```python
import jax
import jax.numpy as jnp
from jax import lax
from jax.sharding import PartitionSpec as P

F = 128
E = 128
K = 128
CHUNKS = 2

PAIR = [(2 * a + y, 2 * b + y) for a, b in ((0, 1), (1, 0), (2, 3), (3, 2)) for y in range(2)]
MID = [(2 * a + y, 2 * b + y) for a, b in ((1, 2), (2, 1)) for y in range(2)]
OUT = [(2 * a + y, 2 * b + y) for a, b in ((1, 0), (2, 3)) for y in range(2)]
INN = [(b, a) for a, b in OUT]
ACROSS = [(2 * z + y, 2 * z + 1 - y) for z in range(4) for y in range(2)]
F32 = jnp.float32
BF16 = jnp.bfloat16


def step(value, pairs):
    return lax.ppermute(value, "tensor", pairs)


def swap(value):
    return lax.ppermute(value, "dp", [(0, 1), (1, 0)])


def place():
    index = lax.axis_index("tensor")
    z, y = index // 2, index % 2
    outer = (z == 0) | (z == 3)
    near = lax.axis_index("dp") == z // 2
    here, beside = z % 2, 1 - z % 2
    far_first = jnp.where(z < 2, 0, 1)
    first = jnp.where(near, here, far_first)
    second = jnp.where(near, beside, 1 - far_first)
    order = (2 * first + y, 2 * first + 1 - y, 2 * second + y, 2 * second + 1 - y)
    return outer, near, order


def gather(own, outer, near):
    e1 = step(own, PAIR)
    m1 = step(own, MID)
    y0 = step(own, ACROSS)
    e2 = step(m1, OUT)
    m2 = step(e1, MID)
    y1 = step(e1, ACROSS)
    b2 = jnp.where(outer, e2, m1)
    e3 = step(m2, OUT)
    y2 = step(b2, ACROSS)
    b3 = jnp.where(outer, e3, m2)
    y3 = step(b3, ACROSS)
    pieces = []
    for close, distant in ((own, b2), (y0, y2), (e1, b3), (y1, y3)):
        kept = jnp.where(near, close, distant)
        other = swap(jnp.where(near, distant, close))
        pieces.append(jnp.concatenate([kept, other], axis=0))
    return pieces


def add(a, b):
    return (a.astype(F32) + b.astype(F32)).astype(BF16)


def scatter(pieces, outer, near):
    close, distant = [], []
    for piece in pieces:
        half = piece.shape[0] // 2
        own, other = piece[:half], swap(piece[half:])
        close.append(jnp.where(near, own, other))
        distant.append(jnp.where(near, other, own))
    b3 = add(distant[2], step(distant[3], ACROSS))
    b2 = add(distant[0], step(distant[1], ACROSS))
    b3 = add(b3, step(b3, INN))
    e1 = add(close[2], step(close[3], ACROSS))
    b2 = add(b2, step(b2, INN))
    e1 = add(e1, step(b3, MID))
    return (
        close[0].astype(F32)
        + step(close[1], ACROSS).astype(F32)
        + step(b2, MID).astype(F32)
        + step(e1, PAIR).astype(F32)
    )


def interact(owned, cotangent, mix_weight, mix_bias, out_weight):
    count = owned.shape[0]
    grid = owned.reshape(count, F, E)
    gram = (jnp.einsum("bfe,bge->bfg", grid, grid, preferred_element_type=F32) / E).astype(BF16)
    pre_act = jnp.einsum("bfg,gh->bfh", gram, mix_weight, preferred_element_type=F32) + mix_bias
    sig = jax.nn.sigmoid(pre_act)
    hidden = (pre_act * sig).astype(BF16)
    compressed = jnp.einsum("bfh,hk->bfk", hidden, out_weight, preferred_element_type=F32).astype(BF16)
    upstream = cotangent.reshape(count, F, K)
    d_hidden = jnp.einsum("bfk,hk->bfh", upstream, out_weight, preferred_element_type=F32)
    out_term = jnp.einsum("bfh,bfk->hk", hidden, upstream, preferred_element_type=F32)
    d_pre = (d_hidden * sig * (1.0 + pre_act * (1.0 - sig))).astype(BF16)
    mix_term = jnp.einsum("bfg,bfh->gh", gram, d_pre, preferred_element_type=F32)
    bias_term = jnp.sum(d_pre.astype(F32), axis=(0, 1))
    d_gram = jnp.einsum("bfh,gh->bfg", d_pre, mix_weight, preferred_element_type=F32)
    d_grid = jnp.einsum("bfg,bge->bfe", d_gram + jnp.swapaxes(d_gram, 1, 2), grid.astype(F32)) / E
    return compressed.reshape(count, F * K), d_grid.astype(BF16).reshape(count, F * E), mix_term, bias_term, out_term


def weight_block(cross_w, at, size):
    return lax.dynamic_slice_in_dim(cross_w, at * size, size, 0)


def linear_grid(own, cross_w, cross_b, spot):
    outer, near, order = spot
    rows, width = own.shape
    pieces = gather(own, outer, near)
    total = None
    for piece, at in zip(pieces, order):
        term = jnp.dot(piece, weight_block(cross_w, at, width), preferred_element_type=F32)
        total = term if total is None else total + term
    return total[:rows] + swap(total[rows:].astype(BF16)).astype(F32) + cross_b


def back_grid(d_linear, cross_w, spot):
    outer, near, order = spot
    width = d_linear.shape[1]
    both = jnp.concatenate([d_linear, swap(d_linear)], axis=0)
    contract = (((1,), (1,)), ((), ()))
    pieces = [
        lax.dot_general(both, weight_block(cross_w, at, width), contract, preferred_element_type=F32).astype(BF16)
        for at in order
    ]
    return scatter(pieces, outer, near)


def linear_any(own, cross_w, cross_b):
    rows = own.shape[0]
    full = lax.all_gather(own, "tensor", axis=1, tiled=True)
    half = full.shape[1] // 2
    core = lax.axis_index("dp")
    kept = lax.dynamic_slice_in_dim(full, core * half, half, 1)
    other = swap(lax.dynamic_slice_in_dim(full, (1 - core) * half, half, 1))
    total = jnp.dot(jnp.concatenate([kept, other], axis=0), cross_w, preferred_element_type=F32)
    return total[:rows] + swap(total[rows:].astype(BF16)).astype(F32) + cross_b


def back_any(d_linear, cross_w):
    rows = d_linear.shape[0]
    both = jnp.concatenate([d_linear, swap(d_linear)], axis=0)
    contract = (((1,), (1,)), ((), ()))
    terms = lax.dot_general(both, cross_w, contract, preferred_element_type=F32).astype(BF16)
    own, other = terms[:rows], swap(terms[rows:])
    first = lax.axis_index("dp") == 0
    full = jnp.concatenate([jnp.where(first, own, other), jnp.where(first, other, own)], axis=1)
    return lax.psum_scatter(full, "tensor", scatter_dimension=1, tiled=True).astype(F32)


def shards(inputs, cross_w, cross_b, mix_weight, mix_bias, out_weight, cotangent):
    local_rows = inputs[0]
    tensor_count, dp_count = lax.axis_size("tensor"), lax.axis_size("dp")
    rows, width = local_rows.shape
    owned_count = rows // tensor_count
    grid = tensor_count == 8
    chunks = CHUNKS if owned_count % (16 * CHUNKS) == 0 else 1
    part = owned_count // chunks
    spot = place() if grid else None
    by_owner = local_rows.reshape(tensor_count, owned_count, width)
    compressed, grads, terms = [], [], []
    for c in range(chunks):
        own = by_owner[:, c * part : (c + 1) * part].reshape(tensor_count * part, width)
        base = own.astype(F32)
        linear = linear_grid(own, cross_w, cross_b, spot) if grid else linear_any(own, cross_w, cross_b)
        crossed = (base * linear + base).astype(BF16)
        owned = lax.all_to_all(crossed, "tensor", split_axis=0, concat_axis=1, tiled=True)
        out, d_owned, mix_term, bias_term, out_term = interact(
            owned, cotangent[0, c * part : (c + 1) * part], mix_weight, mix_bias, out_weight
        )
        compressed.append(out)
        terms.append((mix_term, bias_term, out_term))
        d_crossed = lax.all_to_all(d_owned, "tensor", split_axis=1, concat_axis=0, tiled=True).astype(F32)
        d_linear = (d_crossed * base).astype(BF16)
        back = back_grid(d_linear, cross_w, spot) if grid else back_any(d_linear, cross_w)
        grad = (d_crossed * (linear + 1.0) + back).astype(BF16)
        grads.append(grad.reshape(tensor_count, part, width))
    mix_term, bias_term, out_term = (sum(t[1:], t[0]) for t in zip(*terms))
    row_total = rows * dp_count
    mixed = jnp.concatenate([mix_term, jnp.broadcast_to(bias_term[None] / 8, (8, bias_term.shape[0]))], axis=0)
    mixed_sum, out_sum = lax.psum((mixed.astype(BF16), out_term.astype(BF16)), ("tensor", "dp"))
    mixed_sum = mixed_sum.astype(F32)
    return (
        jnp.concatenate(compressed, axis=0)[None],
        jnp.concatenate(grads, axis=1).reshape(1, rows, width),
        mixed_sum[:F] / row_total,
        jnp.sum(mixed_sum[F:], axis=0) / row_total,
        out_sum.astype(F32) / row_total,
    )


def solution(mesh):
    return jax.shard_map(
        shards,
        mesh=mesh,
        in_specs=(
            P(("groups", "dp"), None, "tensor"),
            P("dp", "tensor"),
            P("tensor"),
            P(),
            P(),
            P(),
            P(("groups", "dp"), "tensor", None),
        ),
        out_specs=(
            P(("groups", "dp"), "tensor", None),
            P(("groups", "dp"), None, "tensor"),
            P("groups", None),
            P("groups"),
            P("groups", None),
        ),
        check_vma=False,
    )
```

```python
import functools

import jax
import jax.numpy as jnp
from jax import lax
from jax.experimental import pallas as pl
from jax.experimental.pallas import tpu as pltpu
from jax.sharding import PartitionSpec as P

F = 128
E = 128
K = 128

PAIR = [(2 * a + y, 2 * b + y) for a, b in ((0, 1), (1, 0), (2, 3), (3, 2)) for y in range(2)]
MID = [(2 * a + y, 2 * b + y) for a, b in ((1, 2), (2, 1)) for y in range(2)]
OUT = [(2 * a + y, 2 * b + y) for a, b in ((1, 0), (2, 3)) for y in range(2)]
INN = [(b, a) for a, b in OUT]
ACROSS = [(2 * z + y, 2 * z + 1 - y) for z in range(4) for y in range(2)]
CROSS = [(2 * z + y, 2 * (z ^ 2) + y) for z in range(4) for y in range(2)]
F32 = jnp.float32
BF16 = jnp.bfloat16


def forward_kernel(count, plan_ref, *refs):
    sources, (w_ref, own_ref, other_ref, x_ref, acc_ref, sems) = refs[: 4 * count], refs[4 * count :]
    at = pl.program_id(0)
    per = pl.num_programs(0) // count
    rows, width = x_ref.shape[1] // 2, x_ref.shape[2]
    depth = width // per
    near = plan_ref[count] == 1
    piece, part = at // per, at % per

    @pl.when(at == 0)
    def _():
        for q in range(count):
            close, distant, close_other, distant_other = sources[4 * q : 4 * q + 4]
            for half, a, b in ((0, close, distant), (1, close_other, distant_other)):
                place = x_ref.at[q, pl.ds(half * rows, rows)]
                pl.when(near)(pltpu.make_async_copy(a, place, sems.at[q, half]).start)
                pl.when(jnp.logical_not(near))(pltpu.make_async_copy(b, place, sems.at[q, half]).start)

    for q in range(count):

        @pl.when((part == 0) & (piece == q))
        def _(q=q):
            for half in range(2):
                place = x_ref.at[q, pl.ds(half * rows, rows)]
                pltpu.make_async_copy(sources[4 * q + 2 * half], place, sems.at[q, half]).wait()

    columns = pl.ds(pl.multiple_of(part * depth, depth), depth)
    term = jnp.dot(x_ref[piece, :, columns], w_ref[...], preferred_element_type=F32)

    @pl.when(at == 0)
    def _():
        acc_ref[...] = term

    @pl.when(at > 0)
    def _():
        acc_ref[...] += term

    @pl.when(at == pl.num_programs(0) - 1)
    def _():
        own_ref[...] = acc_ref[:rows]
        other_ref[...] = acc_ref[rows:].astype(BF16)


def forward_rows(pieces, order, near, cross_w, per=2):
    count = len(pieces)
    rows, width = pieces[0][0].shape
    columns = cross_w.shape[1]
    plan = jnp.stack([*order, near.astype(jnp.int32)])
    half = pl.BlockSpec((rows, columns), lambda s, plan: (0, 0), pipeline_mode=pl.Buffered(1))
    return pl.pallas_call(
        functools.partial(forward_kernel, count),
        grid_spec=pltpu.PrefetchScalarGridSpec(
            num_scalar_prefetch=1,
            grid=(count * per,),
            in_specs=[pl.BlockSpec(memory_space=pl.ANY)] * (4 * count)
            + [pl.BlockSpec((width // per, columns), lambda s, plan: (plan[s // per] * per + s % per, 0))],
            out_specs=[half, half],
            scratch_shapes=[
                pltpu.VMEM((count, 2 * rows, width), BF16),
                pltpu.VMEM((2 * rows, columns), F32),
                pltpu.SemaphoreType.DMA((count, 2)),
            ],
        ),
        out_shape=[jax.ShapeDtypeStruct((rows, columns), F32), jax.ShapeDtypeStruct((rows, columns), BF16)],
        cost_estimate=pl.CostEstimate(
            flops=4 * rows * width * count * columns,
            transcendentals=0,
            bytes_accessed=2 * width * count * columns,
        ),
        name="forward_rows",
    )(plan, *[ref for piece in pieces for ref in piece], cross_w)


def back_kernel(count, plan_ref, own_ref, other_ref, w_ref, *refs):
    outs, x_ref = refs[:-1], refs[-1]
    rows = own_ref.shape[0]
    p = pl.program_id(0)

    @pl.when(p + pl.program_id(1) == 0)
    def _():
        x_ref[:rows] = own_ref[...]
        x_ref[rows:] = other_ref[...]

    contract = (((1,), (1,)), ((), ()))
    term = lax.dot_general(x_ref[...], w_ref[...], contract, preferred_element_type=F32).astype(BF16)
    for q in range(count):

        @pl.when(p == q)
        def _(q=q):
            outs[2 * q][...] = term[:rows]
            outs[2 * q + 1][...] = term[rows:]


def back_part(own, other, order, cross_w, per=2):
    count = len(order)
    rows, width = own.shape
    plan = jnp.stack(list(order))
    tile = width // per
    whole = pl.BlockSpec((rows, width), lambda p, i, plan: (0, 0), pipeline_mode=pl.Buffered(1))

    def out(q):
        return pl.BlockSpec((rows, tile), lambda p, i, plan: (0, jnp.where(p == q, i, jnp.where(p < q, 0, per - 1))))

    return pl.pallas_call(
        functools.partial(back_kernel, count),
        grid_spec=pltpu.PrefetchScalarGridSpec(
            num_scalar_prefetch=1,
            grid=(count, per),
            in_specs=[whole, whole, pl.BlockSpec((tile, width), lambda p, i, plan: (plan[p] * per + i, 0))],
            out_specs=[out(q) for q in range(count) for _ in range(2)],
            scratch_shapes=[pltpu.VMEM((2 * rows, width), BF16)],
        ),
        out_shape=[jax.ShapeDtypeStruct((rows, width), BF16)] * (2 * count),
        cost_estimate=pl.CostEstimate(
            flops=4 * rows * width * count * width,
            transcendentals=0,
            bytes_accessed=2 * width * count * width,
        ),
        name="back_part",
    )(plan, own, other, cross_w)


def interact_kernel(x_ref, up_ref, mix_ref, bias_ref, out_ref, comp_ref, dx_ref, mix_term, bias_term, out_term):
    group = x_ref.shape[1]
    size = x_ref.shape[0] * x_ref.shape[2]

    @pl.when(pl.program_id(0) == 0)
    def _():
        mix_term[...] = jnp.zeros_like(mix_term)
        bias_term[...] = jnp.zeros_like(bias_term)
        out_term[...] = jnp.zeros_like(out_term)

    across = (((1,), (1,)), ((), ()))
    down = (((0,), (0,)), ((), ()))
    grams = []
    xs = [x_ref[:, b].reshape(size, x_ref.shape[3]) for b in range(group)]
    for x in xs:
        gram = lax.dot_general(x, x, across, preferred_element_type=F32) * (1.0 / x.shape[1])
        grams.append(gram.astype(BF16))
    gram = jnp.concatenate(grams, axis=0)
    up = up_ref[...].reshape(group * size, up_ref.shape[2])
    pre = jnp.dot(gram, mix_ref[...], preferred_element_type=F32) + bias_ref[...]
    d_hidden = lax.dot_general(up, out_ref[...], across, preferred_element_type=F32)
    sig = jax.nn.sigmoid(pre)
    hidden = (pre * sig).astype(BF16)
    d_pre = (d_hidden * sig * (1.0 + pre * (1.0 - sig))).astype(BF16)
    comp = jnp.dot(hidden, out_ref[...], preferred_element_type=F32).astype(BF16)
    comp_ref[...] = comp.reshape(comp_ref.shape)
    out_term[...] += lax.dot_general(hidden, up, down, preferred_element_type=F32)
    mix_term[...] += lax.dot_general(gram, d_pre, down, preferred_element_type=F32)
    wide = d_pre.astype(F32)
    bias_term[...] += jnp.sum(wide.reshape(-1, 8, wide.shape[1]), axis=0)
    d_gram = lax.dot_general(d_pre, mix_ref[...], across, preferred_element_type=F32)
    for b in range(group):
        part = d_gram[b * size : (b + 1) * size]
        both = (part + part.T).astype(BF16)
        dx = jnp.dot(both, xs[b], preferred_element_type=F32) * (1.0 / x_ref.shape[3])
        dx_ref[:, b] = dx.astype(BF16).reshape(x_ref.shape[0], x_ref.shape[2], x_ref.shape[3])


def interact_rows(owned, upstream, mix_weight, mix_bias, out_weight, group=8):
    sources, count, parts, e = owned.shape
    f = sources * parts
    hidden, k = out_weight.shape
    rows = pl.BlockSpec((sources, group, parts, e), lambda i: (0, i, 0, 0))
    rows_k = pl.BlockSpec((group, f, k), lambda i: (i, 0, 0))

    def fixed(*shape):
        return pl.BlockSpec(shape, lambda i: (0,) * len(shape))

    return pl.pallas_call(
        interact_kernel,
        grid=(count // group,),
        in_specs=[rows, rows_k, fixed(f, hidden), fixed(1, hidden), fixed(hidden, k)],
        out_specs=[rows_k, rows, fixed(f, hidden), fixed(8, hidden), fixed(hidden, k)],
        out_shape=[
            jax.ShapeDtypeStruct((count, f, k), BF16),
            jax.ShapeDtypeStruct(owned.shape, BF16),
            jax.ShapeDtypeStruct((f, hidden), F32),
            jax.ShapeDtypeStruct((8, hidden), F32),
            jax.ShapeDtypeStruct((hidden, k), F32),
        ],
        cost_estimate=pl.CostEstimate(
            flops=2 * count * f * (2 * f * e + 6 * f * hidden),
            transcendentals=2 * count * f * hidden,
            bytes_accessed=8 * count * f * e,
        ),
        name="interact_rows",
    )(owned, upstream, mix_weight, mix_bias.reshape(1, -1), out_weight)


def step(value, pairs):
    return lax.ppermute(value, "tensor", pairs)


def swap(value):
    return lax.ppermute(value, "dp", [(0, 1), (1, 0)])


def place():
    index = lax.axis_index("tensor")
    z, y = index // 2, index % 2
    outer = (z == 0) | (z == 3)
    near = lax.axis_index("dp") == z // 2
    here, beside = z % 2, 1 - z % 2
    far_first = jnp.where(z < 2, 0, 1)
    first = jnp.where(near, here, far_first)
    second = jnp.where(near, beside, 1 - far_first)
    order = (2 * first + y, 2 * first + 1 - y, 2 * second + y, 2 * second + 1 - y)
    return outer, near, order


def after(value, *others):
    return lax.optimization_barrier((value, *others))[0]


def hold(values, *others):
    return lax.optimization_barrier((*values, *others))[: len(values)]


def add(a, b):
    return (a.astype(F32) + b.astype(F32)).astype(BF16)


def roles(pieces, q, near):
    own, other = pieces[q]
    other = swap(other)
    return jnp.where(near, own, other), jnp.where(near, other, own)


def interact(owned, cotangent, mix_weight, mix_bias, out_weight):
    count = owned.shape[1]
    comp, d_rows, mix_term, bias_term, out_term = interact_rows(
        owned, cotangent.reshape(count, F, K), mix_weight, mix_bias, out_weight
    )
    return comp.reshape(count, F * K), d_rows, mix_term, jnp.sum(bias_term, axis=0), out_term


def exchange_rows(value, owners):
    if value.ndim == 2:
        value = value.reshape(owners, value.shape[0] // owners, value.shape[1] // E, E)
        return lax.all_to_all(value, "tensor", split_axis=0, concat_axis=0, tiled=True)
    value = lax.all_to_all(value, "tensor", split_axis=0, concat_axis=0, tiled=True)
    return value.reshape(value.shape[0] * value.shape[1], value.shape[2] * value.shape[3])


def grid_sum_start(terms):
    mix_term, bias_term, out_term = (x + y for x, y in zip(*terms))
    mixed = jnp.concatenate([mix_term, jnp.broadcast_to(bias_term[None], (8, bias_term.shape[0]))], axis=0)
    wide = out_term.reshape(-1, mixed.shape[1])
    wide = jnp.concatenate([wide, jnp.zeros((mixed.shape[0] - wide.shape[0], wide.shape[1]), F32)], axis=0)
    first = lax.axis_index("dp") == 0
    return jnp.where(first, mixed, wide) + swap(jnp.where(first, wide, mixed).astype(BF16)).astype(F32)


def grid_sum_step(kept, pairs):
    sent = kept.astype(BF16)
    return sent.astype(F32) + step(sent, pairs).astype(F32)


def grid_sum_end(kept, out_shape):
    kept = kept.astype(BF16)
    other = swap(kept)
    first = lax.axis_index("dp") == 0
    mixed, wide = jnp.where(first, kept, other), jnp.where(first, other, kept)
    rows = out_shape[0] * out_shape[1] // kept.shape[1]
    return mixed[:-8].astype(F32), mixed[-8].astype(F32), wide[:rows].astype(F32).reshape(out_shape)


def grid_path(own, cross_w, cross_b, cotangent, small):
    outer, near, order = place()

    def four(close, distant):
        return close, distant, swap(close), swap(distant)

    def linear(pieces, *beside):
        total, other = hold(forward_rows(pieces, order, near, cross_w), *beside)
        return total + swap(other).astype(F32) + cross_b

    def back(d_linear, other, pair, *beside):
        outs = hold(back_part(d_linear, other, [order[q] for q in pair], cross_w), *beside)
        return {pair[0]: outs[:2], pair[1]: outs[2:]}

    def to_owner(c, line):
        base = own[c].astype(F32)
        return exchange_rows((base * line + base).astype(BF16), 8)

    def exchange(pieces, q):
        close, distant = roles(pieces, q, near)
        return distant, close

    def product(c, d_crossed):
        d_linear = (d_crossed.astype(F32) * own[c].astype(F32)).astype(BF16)
        return d_linear, swap(d_linear)

    def finish(c, d_crossed, line, back):
        return (d_crossed.astype(F32) * (line + 1.0) + back).astype(BF16)

    a, b = own
    y0, e1, m1 = step(a, ACROSS), step(a, PAIR), step(a, MID)
    y1, m2 = step(after(e1, y0, m1), ACROSS), step(after(e1, y0, m1), MID)
    e2 = step(after(m1, y0, e1), OUT)
    b2 = jnp.where(outer, e2, m1)
    y2, e3 = step(after(b2, y1, m2), ACROSS), step(after(m2, y1, e2), OUT)
    b3 = jnp.where(outer, e3, m2)
    y3 = step(after(b3, y2), ACROSS)
    first = after(b, y2, e3)
    f1, n1 = step(first, PAIR), step(first, MID)
    pieces = [four(a, b2), four(y0, y2), four(e1, b3), four(y1, y3)]
    x0 = step(after(b, y3, f1), ACROSS)
    x1, n2, f2 = step(after(f1, y3, n1), ACROSS), step(after(f1, y3, n1), MID), step(after(n1, y3, f1), OUT)
    line_a = linear(pieces, x0, x1, n2, f2)
    b2 = jnp.where(outer, f2, n1)
    x2, f3 = step(after(b2, x0, x1, n2), ACROSS), step(after(n2, x1, f2), OUT)
    owned_a = to_owner(0, after(line_a, b2))
    b3 = jnp.where(outer, f3, n2)
    x3 = step(after(b3, x2), ACROSS)
    out_a, d_rows_a, *terms_a = interact(after(owned_a, x2, f3), cotangent[0], *small)
    back_a = exchange_rows(d_rows_a, 8)
    pieces = [four(after(b, d_rows_a), b2), four(x0, x2), four(f1, b3), four(x1, x3)]
    line_b = linear(pieces, back_a)
    owned_b = to_owner(1, line_b)
    d_linear, other = product(0, back_a)
    part = back(after(d_linear, line_b), other, (3, 2), owned_b)
    distant3, close3 = exchange(part, 3)
    g3, h3 = step(distant3, ACROSS), step(close3, ACROSS)
    out_b, d_rows_b, *terms_b = interact(after(owned_b, distant3, close3), cotangent[1], *small)
    back_b = exchange_rows(d_rows_b, 8)
    second = back(after(d_linear, d_rows_b), other, (1, 0), g3, h3)
    h3_a = h3
    distant2, close2 = exchange(part, 2)
    distant1, close1 = exchange(second, 1)
    b3 = add(distant2, after(g3, distant1))
    k3 = step(b3, INN)
    g1, h1 = step(after(distant1, h3), ACROSS), step(after(close1, h3), ACROSS)
    kept = grid_sum_step(grid_sum_start((terms_a, terms_b)), ACROSS)
    d_next, other = product(1, back_b)
    part = back(after(d_next, second[1][0]), other, (3, 2), g1, k3, kept)
    kept, k3, g1_a = hold((kept, k3, g1), part[3][0])
    close_a, distant0 = roles(second, 0, near)
    distant3, close3 = exchange(part, 3)
    g3, h3 = step(distant3, ACROSS), step(close3, ACROSS)
    h1_a = h1
    b3, b2, e1 = add(b3, k3), add(distant0, g1_a), add(close2, h3_a)
    k2, r2 = step(b3, MID), step(b2, INN)
    kept = grid_sum_step(kept, PAIR)
    second = back(after(d_next, part[3][0], distant3), other, (1, 0), h1, k2, r2, kept)
    kept, k2, r2 = hold((kept, k2, r2), second[1][0])
    distant1, close1 = exchange(second, 1)
    g1, h1 = step(after(distant1, g3), ACROSS), step(after(close1, g3), ACROSS)
    distant2, close2 = exchange(part, 2)
    b3 = add(distant2, g3)
    k3 = step(b3, INN)
    r0, r1 = step(add(b2, r2), MID), step(add(e1, k2), PAIR)
    kept = grid_sum_step(after(kept, k3), CROSS)
    k2 = step(after(add(b3, k3), r0), MID)
    close0, distant0 = roles(second, 0, near)
    sum_a = close_a.astype(F32) + h1_a.astype(F32) + r0.astype(F32) + r1.astype(F32)
    b2 = add(distant0, g1)
    r2 = step(b2, INN)
    e1 = add(add(close2, h3), k2)
    r1 = step(e1, PAIR)
    r0 = step(add(b2, r2), MID)
    sums = grid_sum_end(after(kept, r2), terms_a[2].shape)
    grad_a = finish(0, back_a, line_a, after(sum_a, r2))
    sum_b = close0.astype(F32) + h1.astype(F32) + r0.astype(F32) + r1.astype(F32)
    grad_b = finish(1, back_b, line_b, sum_b)
    return (out_a, out_b), sums, (grad_a, grad_b)


def linear_any(own, cross_w, cross_b):
    rows = own.shape[0]
    full = lax.all_gather(own, "tensor", axis=1, tiled=True)
    half = full.shape[1] // 2
    core = lax.axis_index("dp")
    kept = lax.dynamic_slice_in_dim(full, core * half, half, 1)
    other = swap(lax.dynamic_slice_in_dim(full, (1 - core) * half, half, 1))
    total = jnp.dot(jnp.concatenate([kept, other], axis=0), cross_w, preferred_element_type=F32)
    return total[:rows] + swap(total[rows:].astype(BF16)).astype(F32) + cross_b


def back_any(d_linear, cross_w):
    rows = d_linear.shape[0]
    both = jnp.concatenate([d_linear, swap(d_linear)], axis=0)
    contract = (((1,), (1,)), ((), ()))
    terms = lax.dot_general(both, cross_w, contract, preferred_element_type=F32).astype(BF16)
    own, other = terms[:rows], swap(terms[rows:])
    first = lax.axis_index("dp") == 0
    full = jnp.concatenate([jnp.where(first, own, other), jnp.where(first, other, own)], axis=1)
    return lax.psum_scatter(full, "tensor", scatter_dimension=1, tiled=True).astype(F32)


def shards(inputs, cross_w, cross_b, mix_weight, mix_bias, out_weight, cotangent):
    own = inputs[0]
    rows, width = own.shape
    tensor_count, dp_count = lax.axis_size("tensor"), lax.axis_size("dp")
    small = mix_weight, mix_bias, out_weight
    if tensor_count == 8:
        half = rows // tensor_count // 2
        by_owner = own.reshape(tensor_count, 2 * half, width)
        halves = [by_owner[:, c * half : (c + 1) * half].reshape(rows // 2, width) for c in range(2)]
        up = [cotangent[0, c * half : (c + 1) * half] for c in range(2)]
        compressed, sums, grads = grid_path(halves, cross_w, cross_b, up, small)
        compressed = jnp.concatenate(compressed, axis=0)
        grads = [grad.reshape(tensor_count, half, width) for grad in grads]
        grad = jnp.concatenate(grads, axis=1).reshape(rows, width)
    else:
        base = own.astype(F32)
        linear = linear_any(own, cross_w, cross_b)
        owned = exchange_rows((base * linear + base).astype(BF16), tensor_count)
        compressed, d_rows, *terms = interact(owned, cotangent[0], *small)
        d_crossed = exchange_rows(d_rows, tensor_count).astype(F32)
        back = back_any((d_crossed * base).astype(BF16), cross_w)
        grad = (d_crossed * (linear + 1.0) + back).astype(BF16)
        sums = [value.astype(F32) for value in lax.psum([t.astype(BF16) for t in terms], ("tensor", "dp"))]
    row_total = rows * dp_count
    return compressed[None], grad[None], *(value / row_total for value in sums)


def solution(mesh):
    return jax.shard_map(
        shards,
        mesh=mesh,
        in_specs=(
            P(("groups", "dp"), None, "tensor"),
            P("dp", "tensor"),
            P("tensor"),
            P(),
            P(),
            P(),
            P(("groups", "dp"), "tensor", None),
        ),
        out_specs=(
            P(("groups", "dp"), "tensor", None),
            P(("groups", "dp"), None, "tensor"),
            P("groups", None),
            P("groups"),
            P("groups", None),
        ),
        check_vma=False,
    )
```

```python
import functools

import jax
import jax.numpy as jnp
from jax import lax
from jax.experimental import pallas as pl
from jax.experimental.pallas import tpu as pltpu
from jax.sharding import PartitionSpec as P

F = 128
E = 128
K = 128

PAIR = [(2 * a + y, 2 * b + y) for a, b in ((0, 1), (1, 0), (2, 3), (3, 2)) for y in range(2)]
MID = [(2 * a + y, 2 * b + y) for a, b in ((1, 2), (2, 1)) for y in range(2)]
OUT = [(2 * a + y, 2 * b + y) for a, b in ((1, 0), (2, 3)) for y in range(2)]
INN = [(b, a) for a, b in OUT]
ACROSS = [(2 * z + y, 2 * z + 1 - y) for z in range(4) for y in range(2)]
CROSS = [(2 * z + y, 2 * (z ^ 2) + y) for z in range(4) for y in range(2)]
F32 = jnp.float32
BF16 = jnp.bfloat16


def forward_kernel(count, plan_ref, *refs):
    sources, (w_ref, own_ref, other_ref, x_ref, acc_ref, sems) = refs[: 4 * count], refs[4 * count :]
    at = pl.program_id(0)
    per = pl.num_programs(0) // count
    rows, width = x_ref.shape[1] // 2, x_ref.shape[2]
    depth = width // per
    near = plan_ref[count] == 1
    piece, part = at // per, at % per

    @pl.when(at == 0)
    def _():
        for q in range(count):
            close, distant, close_other, distant_other = sources[4 * q : 4 * q + 4]
            for half, a, b in ((0, close, distant), (1, close_other, distant_other)):
                place = x_ref.at[q, pl.ds(half * rows, rows)]
                pl.when(near)(pltpu.make_async_copy(a, place, sems.at[q, half]).start)
                pl.when(jnp.logical_not(near))(pltpu.make_async_copy(b, place, sems.at[q, half]).start)

    for q in range(count):

        @pl.when((part == 0) & (piece == q))
        def _(q=q):
            for half in range(2):
                place = x_ref.at[q, pl.ds(half * rows, rows)]
                pltpu.make_async_copy(sources[4 * q + 2 * half], place, sems.at[q, half]).wait()

    columns = pl.ds(pl.multiple_of(part * depth, depth), depth)
    term = jnp.dot(x_ref[piece, :, columns], w_ref[...], preferred_element_type=F32)

    @pl.when(at == 0)
    def _():
        acc_ref[...] = term

    @pl.when(at > 0)
    def _():
        acc_ref[...] += term

    @pl.when(at == pl.num_programs(0) - 1)
    def _():
        own_ref[...] = acc_ref[:rows]
        other_ref[...] = acc_ref[rows:].astype(BF16)


def forward_rows(pieces, order, near, cross_w, per=1):
    count = len(pieces)
    rows, width = pieces[0][0].shape
    columns = cross_w.shape[1]
    plan = jnp.stack([*order, near.astype(jnp.int32)])
    half = pl.BlockSpec((rows, columns), lambda s, plan: (0, 0), pipeline_mode=pl.Buffered(1))
    return pl.pallas_call(
        functools.partial(forward_kernel, count),
        grid_spec=pltpu.PrefetchScalarGridSpec(
            num_scalar_prefetch=1,
            grid=(count * per,),
            in_specs=[pl.BlockSpec(memory_space=pl.ANY)] * (4 * count)
            + [pl.BlockSpec((width // per, columns), lambda s, plan: (plan[s // per] * per + s % per, 0))],
            out_specs=[half, half],
            scratch_shapes=[
                pltpu.VMEM((count, 2 * rows, width), BF16),
                pltpu.VMEM((2 * rows, columns), F32),
                pltpu.SemaphoreType.DMA((count, 2)),
            ],
        ),
        out_shape=[jax.ShapeDtypeStruct((rows, columns), F32), jax.ShapeDtypeStruct((rows, columns), BF16)],
        cost_estimate=pl.CostEstimate(
            flops=4 * rows * width * count * columns,
            transcendentals=0,
            bytes_accessed=2 * width * count * columns,
        ),
        name="forward_rows",
    )(plan, *[ref for piece in pieces for ref in piece], cross_w)


def back_kernel(count, plan_ref, own_ref, other_ref, w_ref, *refs):
    outs, x_ref = refs[:-1], refs[-1]
    rows = own_ref.shape[0]
    p = pl.program_id(0)

    @pl.when(p + pl.program_id(1) == 0)
    def _():
        x_ref[:rows] = own_ref[...]
        x_ref[rows:] = other_ref[...]

    contract = (((1,), (1,)), ((), ()))
    term = lax.dot_general(x_ref[...], w_ref[...], contract, preferred_element_type=F32).astype(BF16)
    for q in range(count):

        @pl.when(p == q)
        def _(q=q):
            outs[2 * q][...] = term[:rows]
            outs[2 * q + 1][...] = term[rows:]


def back_part(own, other, order, cross_w, per=2):
    count = len(order)
    rows, width = own.shape
    plan = jnp.stack(list(order))
    tile = width // per
    whole = pl.BlockSpec((rows, width), lambda p, i, plan: (0, 0), pipeline_mode=pl.Buffered(1))

    def out(q):
        return pl.BlockSpec((rows, tile), lambda p, i, plan: (0, jnp.where(p == q, i, jnp.where(p < q, 0, per - 1))))

    return pl.pallas_call(
        functools.partial(back_kernel, count),
        grid_spec=pltpu.PrefetchScalarGridSpec(
            num_scalar_prefetch=1,
            grid=(count, per),
            in_specs=[whole, whole, pl.BlockSpec((tile, width), lambda p, i, plan: (plan[p] * per + i, 0))],
            out_specs=[out(q) for q in range(count) for _ in range(2)],
            scratch_shapes=[pltpu.VMEM((2 * rows, width), BF16)],
        ),
        out_shape=[jax.ShapeDtypeStruct((rows, width), BF16)] * (2 * count),
        cost_estimate=pl.CostEstimate(
            flops=4 * rows * width * count * width,
            transcendentals=0,
            bytes_accessed=2 * width * count * width,
        ),
        name="back_part",
    )(plan, own, other, cross_w)


def interact_kernel(x_ref, up_ref, mix_ref, bias_ref, out_ref, comp_ref, dx_ref, mix_term, bias_term, out_term):
    group = x_ref.shape[1]
    size = x_ref.shape[0] * x_ref.shape[2]

    @pl.when(pl.program_id(0) == 0)
    def _():
        mix_term[...] = jnp.zeros_like(mix_term)
        bias_term[...] = jnp.zeros_like(bias_term)
        out_term[...] = jnp.zeros_like(out_term)

    across = (((1,), (1,)), ((), ()))
    down = (((0,), (0,)), ((), ()))
    grams = []
    xs = [x_ref[:, b].reshape(size, x_ref.shape[3]) for b in range(group)]
    for x in xs:
        gram = lax.dot_general(x, x, across, preferred_element_type=F32) * (1.0 / x.shape[1])
        grams.append(gram.astype(BF16))
    gram = jnp.concatenate(grams, axis=0)
    up = up_ref[...].reshape(group * size, up_ref.shape[2])
    pre = jnp.dot(gram, mix_ref[...], preferred_element_type=F32) + bias_ref[...]
    d_hidden = lax.dot_general(up, out_ref[...], across, preferred_element_type=F32)
    sig = jax.nn.sigmoid(pre)
    hidden = (pre * sig).astype(BF16)
    d_pre = (d_hidden * sig * (1.0 + pre * (1.0 - sig))).astype(BF16)
    comp = jnp.dot(hidden, out_ref[...], preferred_element_type=F32).astype(BF16)
    comp_ref[...] = comp.reshape(comp_ref.shape)
    out_term[...] += lax.dot_general(hidden, up, down, preferred_element_type=F32)
    mix_term[...] += lax.dot_general(gram, d_pre, down, preferred_element_type=F32)
    wide = d_pre.astype(F32)
    bias_term[...] += jnp.sum(wide.reshape(-1, 8, wide.shape[1]), axis=0)
    d_gram = lax.dot_general(d_pre, mix_ref[...], across, preferred_element_type=F32)
    for b in range(group):
        part = d_gram[b * size : (b + 1) * size]
        both = (part + part.T).astype(BF16)
        dx = jnp.dot(both, xs[b], preferred_element_type=F32) * (1.0 / x_ref.shape[3])
        dx_ref[:, b] = dx.astype(BF16).reshape(x_ref.shape[0], x_ref.shape[2], x_ref.shape[3])


def interact_rows(owned, upstream, mix_weight, mix_bias, out_weight, group=8):
    sources, count, parts, e = owned.shape
    f = sources * parts
    hidden, k = out_weight.shape
    rows = pl.BlockSpec((sources, group, parts, e), lambda i: (0, i, 0, 0))
    rows_k = pl.BlockSpec((group, f, k), lambda i: (i, 0, 0))

    def fixed(*shape):
        return pl.BlockSpec(shape, lambda i: (0,) * len(shape))

    return pl.pallas_call(
        interact_kernel,
        grid=(count // group,),
        in_specs=[rows, rows_k, fixed(f, hidden), fixed(1, hidden), fixed(hidden, k)],
        out_specs=[rows_k, rows, fixed(f, hidden), fixed(8, hidden), fixed(hidden, k)],
        out_shape=[
            jax.ShapeDtypeStruct((count, f, k), BF16),
            jax.ShapeDtypeStruct(owned.shape, BF16),
            jax.ShapeDtypeStruct((f, hidden), F32),
            jax.ShapeDtypeStruct((8, hidden), F32),
            jax.ShapeDtypeStruct((hidden, k), F32),
        ],
        cost_estimate=pl.CostEstimate(
            flops=2 * count * f * (2 * f * e + 6 * f * hidden),
            transcendentals=2 * count * f * hidden,
            bytes_accessed=8 * count * f * e,
        ),
        name="interact_rows",
    )(owned, upstream, mix_weight, mix_bias.reshape(1, -1), out_weight)


def step(value, pairs):
    return lax.ppermute(value, "tensor", pairs)


def swap(value):
    return lax.ppermute(value, "dp", [(0, 1), (1, 0)])


def place():
    index = lax.axis_index("tensor")
    z, y = index // 2, index % 2
    outer = (z == 0) | (z == 3)
    near = lax.axis_index("dp") == z // 2
    here, beside = z % 2, 1 - z % 2
    far_first = jnp.where(z < 2, 0, 1)
    first = jnp.where(near, here, far_first)
    second = jnp.where(near, beside, 1 - far_first)
    order = (2 * first + y, 2 * first + 1 - y, 2 * second + y, 2 * second + 1 - y)
    return outer, near, order


def after(value, *others):
    return lax.optimization_barrier((value, *others))[0]


def hold(values, *others):
    return lax.optimization_barrier((*values, *others))[: len(values)]


def add(a, b):
    return (a.astype(F32) + b.astype(F32)).astype(BF16)


def roles(pieces, q, near):
    own, other = pieces[q]
    other = swap(other)
    return jnp.where(near, own, other), jnp.where(near, other, own)


def interact(owned, cotangent, mix_weight, mix_bias, out_weight):
    count = owned.shape[1]
    comp, d_rows, mix_term, bias_term, out_term = interact_rows(
        owned, cotangent.reshape(count, F, K), mix_weight, mix_bias, out_weight
    )
    return comp.reshape(count, F * K), d_rows, mix_term, jnp.sum(bias_term, axis=0), out_term


def exchange_rows(value, owners):
    if value.ndim == 2:
        value = value.reshape(owners, value.shape[0] // owners, value.shape[1] // E, E)
        return lax.all_to_all(value, "tensor", split_axis=0, concat_axis=0, tiled=True)
    value = lax.all_to_all(value, "tensor", split_axis=0, concat_axis=0, tiled=True)
    return value.reshape(value.shape[0] * value.shape[1], value.shape[2] * value.shape[3])


def grid_sum_start(terms):
    mix_term, bias_term, out_term = (x + y for x, y in zip(*terms))
    mixed = jnp.concatenate([mix_term, jnp.broadcast_to(bias_term[None], (8, bias_term.shape[0]))], axis=0)
    wide = out_term.reshape(-1, mixed.shape[1])
    wide = jnp.concatenate([wide, jnp.zeros((mixed.shape[0] - wide.shape[0], wide.shape[1]), F32)], axis=0)
    first = lax.axis_index("dp") == 0
    return jnp.where(first, mixed, wide) + swap(jnp.where(first, wide, mixed).astype(BF16)).astype(F32)


def grid_sum_step(kept, pairs):
    sent = kept.astype(BF16)
    return sent.astype(F32) + step(sent, pairs).astype(F32)


def grid_sum_end(kept, out_shape):
    kept = kept.astype(BF16)
    other = swap(kept)
    first = lax.axis_index("dp") == 0
    mixed, wide = jnp.where(first, kept, other), jnp.where(first, other, kept)
    rows = out_shape[0] * out_shape[1] // kept.shape[1]
    return mixed[:-8].astype(F32), mixed[-8].astype(F32), wide[:rows].astype(F32).reshape(out_shape)


def grid_path(own, cross_w, cross_b, cotangent, small):
    outer, near, order = place()

    def four(close, distant):
        return close, distant, swap(close), swap(distant)

    def linear(pieces, *beside):
        total, other = hold(forward_rows(pieces, order, near, cross_w), *beside)
        return total + swap(other).astype(F32) + cross_b

    def back(d_linear, other, pair, *beside):
        outs = hold(back_part(d_linear, other, [order[q] for q in pair], cross_w), *beside)
        return {pair[0]: outs[:2], pair[1]: outs[2:]}

    def to_owner(c, line):
        base = own[c].astype(F32)
        return exchange_rows((base * line + base).astype(BF16), 8)

    def exchange(pieces, q):
        close, distant = roles(pieces, q, near)
        return distant, close

    def product(c, d_crossed):
        d_linear = (d_crossed.astype(F32) * own[c].astype(F32)).astype(BF16)
        return d_linear, swap(d_linear)

    def finish(c, d_crossed, line, back):
        return (d_crossed.astype(F32) * (line + 1.0) + back).astype(BF16)

    a, b = own
    y0, e1, m1 = step(a, ACROSS), step(a, PAIR), step(a, MID)
    y1, m2 = step(after(e1, y0, m1), ACROSS), step(after(e1, y0, m1), MID)
    e2 = step(after(m1, y0, e1), OUT)
    b2 = jnp.where(outer, e2, m1)
    y2, e3 = step(after(b2, y1, m2), ACROSS), step(after(m2, y1, e2), OUT)
    b3 = jnp.where(outer, e3, m2)
    y3 = step(after(b3, y2), ACROSS)
    first = after(b, y2, e3)
    f1, n1 = step(first, PAIR), step(first, MID)
    pieces = [four(a, b2), four(y0, y2), four(e1, b3), four(y1, y3)]
    x0 = step(after(b, y3, f1), ACROSS)
    x1, n2, f2 = step(after(f1, y3, n1), ACROSS), step(after(f1, y3, n1), MID), step(after(n1, y3, f1), OUT)
    line_a = linear(pieces, x0, x1, n2, f2)
    b2 = jnp.where(outer, f2, n1)
    x2, f3 = step(after(b2, x0, x1, n2), ACROSS), step(after(n2, x1, f2), OUT)
    owned_a = to_owner(0, after(line_a, b2))
    b3 = jnp.where(outer, f3, n2)
    x3 = step(after(b3, x2), ACROSS)
    out_a, d_rows_a, *terms_a = interact(after(owned_a, x2, f3), cotangent[0], *small)
    back_a = exchange_rows(d_rows_a, 8)
    pieces = [four(after(b, d_rows_a), b2), four(x0, x2), four(f1, b3), four(x1, x3)]
    line_b = linear(pieces, back_a)
    owned_b = to_owner(1, line_b)
    d_linear, other = product(0, back_a)
    part = back(after(d_linear, line_b), other, (3, 1), owned_b)
    distant3, close3 = exchange(part, 3)
    distant1, close1 = exchange(part, 1)
    g3, g1 = step(distant3, ACROSS), step(after(distant1, distant3), ACROSS)
    out_b, d_rows_b, *terms_b = hold(interact(after(owned_b, distant3, distant1), cotangent[1], *small), g3)
    back_b = exchange_rows(d_rows_b, 8)
    kept = grid_sum_start((terms_a, terms_b))
    second = back(after(d_linear, d_rows_b), other, (2, 0), g3, back_b)
    h3, h1 = step(after(close3, g3), ACROSS), step(after(close1, g3), ACROSS)
    distant2, close2 = exchange(second, 2)
    close0, distant0 = roles(second, 0, near)
    b3 = add(distant2, g3)
    b2 = add(after(distant0, b3), g1)
    k3, r2 = step(b3, INN), step(b2, INN)
    kept = grid_sum_step(after(kept, second[2][0]), PAIR)
    d_next, other = product(1, back_b)
    part = back(after(d_next, b3), other, (3, 1), k3, h3, kept)
    distant3, close3 = exchange(part, 3)
    distant1, close1 = exchange(part, 1)
    g3, g1 = step(after(distant3, h3), ACROSS), step(after(distant1, distant3), ACROSS)
    k3, kept = hold((k3, kept), distant3, distant1)
    b3, e1 = add(b3, k3), add(close2, h3)
    k2 = step(b3, MID)
    sent = kept.astype(BF16)
    got = step(sent, CROSS)
    sum_a = close0.astype(F32) + h1.astype(F32)
    second = back(after(d_next, distant3, distant1), other, (2, 0), g3, g1, h1, r2, k2)
    h3, h1 = step(after(close3, g3), ACROSS), step(after(close1, g3), ACROSS)
    distant2, close2 = exchange(second, 2)
    close0, distant0 = roles(second, 0, near)
    b3 = add(distant2, g3)
    k3 = step(b3, INN)
    k2, r2, got = hold((k2, r2, got), b3)
    sent = (sent.astype(F32) + got.astype(F32)).astype(BF16)
    got = step(sent, ACROSS)
    r0_a = step(add(b2, r2), MID)
    e1 = add(e1, k2)
    b2 = add(after(distant0, b3), g1)
    r2 = step(b2, INN)
    b3 = add(b3, k3)
    k2 = step(b3, MID)
    r1_a = step(after(e1, b2), PAIR)
    e1 = add(add(close2, h3), k2)
    r1 = step(e1, PAIR)
    r0 = step(add(b2, r2), MID)
    r0_a, r1_a, got = hold((r0_a, r1_a, got), r2, k2)
    kept = sent.astype(F32) + got.astype(F32)
    sum_a = sum_a + r0_a.astype(F32) + r1_a.astype(F32)
    sums = grid_sum_end(kept, terms_a[2].shape)
    sum_b = close0.astype(F32) + h1.astype(F32) + r0.astype(F32) + r1.astype(F32)
    grad_a = finish(0, back_a, line_a, sum_a)
    grad_b = finish(1, back_b, line_b, sum_b)
    return (out_a, out_b), sums, (grad_a, grad_b)


def linear_any(own, cross_w, cross_b):
    rows = own.shape[0]
    full = lax.all_gather(own, "tensor", axis=1, tiled=True)
    half = full.shape[1] // 2
    core = lax.axis_index("dp")
    kept = lax.dynamic_slice_in_dim(full, core * half, half, 1)
    other = swap(lax.dynamic_slice_in_dim(full, (1 - core) * half, half, 1))
    total = jnp.dot(jnp.concatenate([kept, other], axis=0), cross_w, preferred_element_type=F32)
    return total[:rows] + swap(total[rows:].astype(BF16)).astype(F32) + cross_b


def back_any(d_linear, cross_w):
    rows = d_linear.shape[0]
    both = jnp.concatenate([d_linear, swap(d_linear)], axis=0)
    contract = (((1,), (1,)), ((), ()))
    terms = lax.dot_general(both, cross_w, contract, preferred_element_type=F32).astype(BF16)
    own, other = terms[:rows], swap(terms[rows:])
    first = lax.axis_index("dp") == 0
    full = jnp.concatenate([jnp.where(first, own, other), jnp.where(first, other, own)], axis=1)
    return lax.psum_scatter(full, "tensor", scatter_dimension=1, tiled=True).astype(F32)


def shards(inputs, cross_w, cross_b, mix_weight, mix_bias, out_weight, cotangent):
    own = inputs[0]
    rows, width = own.shape
    tensor_count, dp_count = lax.axis_size("tensor"), lax.axis_size("dp")
    small = mix_weight, mix_bias, out_weight
    if tensor_count == 8:
        half = rows // tensor_count // 2
        by_owner = own.reshape(tensor_count, 2 * half, width)
        halves = [by_owner[:, c * half : (c + 1) * half].reshape(rows // 2, width) for c in range(2)]
        up = [cotangent[0, c * half : (c + 1) * half] for c in range(2)]
        compressed, sums, grads = grid_path(halves, cross_w, cross_b, up, small)
        compressed = jnp.concatenate(compressed, axis=0)
        grads = [grad.reshape(tensor_count, half, width) for grad in grads]
        grad = jnp.concatenate(grads, axis=1).reshape(rows, width)
    else:
        base = own.astype(F32)
        linear = linear_any(own, cross_w, cross_b)
        owned = exchange_rows((base * linear + base).astype(BF16), tensor_count)
        compressed, d_rows, *terms = interact(owned, cotangent[0], *small)
        d_crossed = exchange_rows(d_rows, tensor_count).astype(F32)
        back = back_any((d_crossed * base).astype(BF16), cross_w)
        grad = (d_crossed * (linear + 1.0) + back).astype(BF16)
        sums = [value.astype(F32) for value in lax.psum([t.astype(BF16) for t in terms], ("tensor", "dp"))]
    row_total = rows * dp_count
    return compressed[None], grad[None], *(value / row_total for value in sums)


def solution(mesh):
    return jax.shard_map(
        shards,
        mesh=mesh,
        in_specs=(
            P(("groups", "dp"), None, "tensor"),
            P("dp", "tensor"),
            P("tensor"),
            P(),
            P(),
            P(),
            P(("groups", "dp"), "tensor", None),
        ),
        out_specs=(
            P(("groups", "dp"), "tensor", None),
            P(("groups", "dp"), None, "tensor"),
            P("groups", None),
            P("groups"),
            P("groups", None),
        ),
        check_vma=False,
    )
```

```python
import functools

import jax
import jax.numpy as jnp
from jax import lax
from jax.experimental import pallas as pl
from jax.experimental.pallas import tpu as pltpu
from jax.sharding import PartitionSpec as P

F = 128
E = 128
K = 128

PAIR = [(2 * a + y, 2 * b + y) for a, b in ((0, 1), (1, 0), (2, 3), (3, 2)) for y in range(2)]
MID = [(2 * a + y, 2 * b + y) for a, b in ((1, 2), (2, 1)) for y in range(2)]
OUT = [(2 * a + y, 2 * b + y) for a, b in ((1, 0), (2, 3)) for y in range(2)]
INN = [(b, a) for a, b in OUT]
ACROSS = [(2 * z + y, 2 * z + 1 - y) for z in range(4) for y in range(2)]
CROSS = [(2 * z + y, 2 * (z ^ 2) + y) for z in range(4) for y in range(2)]
F32 = jnp.float32
BF16 = jnp.bfloat16


def forward_kernel(count, plan_ref, *refs):
    sources, (w_ref, own_ref, other_ref, x_ref, acc_ref, sems) = refs[: 4 * count], refs[4 * count :]
    at = pl.program_id(0)
    per = pl.num_programs(0) // count
    rows, width = x_ref.shape[1] // 2, x_ref.shape[2]
    depth = width // per
    near = plan_ref[count] == 1
    piece, part = at // per, at % per

    @pl.when(at == 0)
    def _():
        for q in range(count):
            close, distant, close_other, distant_other = sources[4 * q : 4 * q + 4]
            for half, a, b in ((0, close, distant), (1, close_other, distant_other)):
                place = x_ref.at[q, pl.ds(half * rows, rows)]
                pl.when(near)(pltpu.make_async_copy(a, place, sems.at[q, half]).start)
                pl.when(jnp.logical_not(near))(pltpu.make_async_copy(b, place, sems.at[q, half]).start)

    for q in range(count):

        @pl.when((part == 0) & (piece == q))
        def _(q=q):
            for half in range(2):
                place = x_ref.at[q, pl.ds(half * rows, rows)]
                pltpu.make_async_copy(sources[4 * q + 2 * half], place, sems.at[q, half]).wait()

    columns = pl.ds(pl.multiple_of(part * depth, depth), depth)
    term = jnp.dot(x_ref[piece, :, columns], w_ref[...], preferred_element_type=F32)

    @pl.when(at == 0)
    def _():
        acc_ref[...] = term

    @pl.when(at > 0)
    def _():
        acc_ref[...] += term

    @pl.when(at == pl.num_programs(0) - 1)
    def _():
        own_ref[...] = acc_ref[:rows]
        other_ref[...] = acc_ref[rows:].astype(BF16)


def forward_rows(pieces, order, near, cross_w, per=1):
    count = len(pieces)
    rows, width = pieces[0][0].shape
    columns = cross_w.shape[1]
    plan = jnp.stack([*order, near.astype(jnp.int32)])
    half = pl.BlockSpec((rows, columns), lambda s, plan: (0, 0), pipeline_mode=pl.Buffered(1))
    return pl.pallas_call(
        functools.partial(forward_kernel, count),
        grid_spec=pltpu.PrefetchScalarGridSpec(
            num_scalar_prefetch=1,
            grid=(count * per,),
            in_specs=[pl.BlockSpec(memory_space=pl.ANY)] * (4 * count)
            + [pl.BlockSpec((width // per, columns), lambda s, plan: (plan[s // per] * per + s % per, 0))],
            out_specs=[half, half],
            scratch_shapes=[
                pltpu.VMEM((count, 2 * rows, width), BF16),
                pltpu.VMEM((2 * rows, columns), F32),
                pltpu.SemaphoreType.DMA((count, 2)),
            ],
        ),
        out_shape=[jax.ShapeDtypeStruct((rows, columns), F32), jax.ShapeDtypeStruct((rows, columns), BF16)],
        cost_estimate=pl.CostEstimate(
            flops=4 * rows * width * count * columns,
            transcendentals=0,
            bytes_accessed=2 * width * count * columns,
        ),
        name="forward_rows",
    )(plan, *[ref for piece in pieces for ref in piece], cross_w)


def back_kernel(count, plan_ref, own_ref, other_ref, w_ref, *refs):
    outs, x_ref = refs[:-1], refs[-1]
    rows = own_ref.shape[0]
    p = pl.program_id(0)

    @pl.when(p + pl.program_id(1) == 0)
    def _():
        x_ref[:rows] = own_ref[...]
        x_ref[rows:] = other_ref[...]

    contract = (((1,), (1,)), ((), ()))
    term = lax.dot_general(x_ref[...], w_ref[...], contract, preferred_element_type=F32).astype(BF16)
    for q in range(count):

        @pl.when(p == q)
        def _(q=q):
            outs[2 * q][...] = term[:rows]
            outs[2 * q + 1][...] = term[rows:]


def back_part(own, other, order, cross_w, per=2):
    count = len(order)
    rows, width = own.shape
    plan = jnp.stack(list(order))
    tile = width // per
    whole = pl.BlockSpec((rows, width), lambda p, i, plan: (0, 0), pipeline_mode=pl.Buffered(1))

    def out(q):
        return pl.BlockSpec((rows, tile), lambda p, i, plan: (0, jnp.where(p == q, i, jnp.where(p < q, 0, per - 1))))

    return pl.pallas_call(
        functools.partial(back_kernel, count),
        grid_spec=pltpu.PrefetchScalarGridSpec(
            num_scalar_prefetch=1,
            grid=(count, per),
            in_specs=[whole, whole, pl.BlockSpec((tile, width), lambda p, i, plan: (plan[p] * per + i, 0))],
            out_specs=[out(q) for q in range(count) for _ in range(2)],
            scratch_shapes=[pltpu.VMEM((2 * rows, width), BF16)],
        ),
        out_shape=[jax.ShapeDtypeStruct((rows, width), BF16)] * (2 * count),
        cost_estimate=pl.CostEstimate(
            flops=4 * rows * width * count * width,
            transcendentals=0,
            bytes_accessed=2 * width * count * width,
        ),
        name="back_part",
    )(plan, own, other, cross_w)


def interact_kernel(x_ref, up_ref, mix_ref, bias_ref, out_ref, comp_ref, dx_ref, mix_term, bias_term, out_term):
    group = x_ref.shape[1]
    size = x_ref.shape[0] * x_ref.shape[2]

    @pl.when(pl.program_id(0) == 0)
    def _():
        mix_term[...] = jnp.zeros_like(mix_term)
        bias_term[...] = jnp.zeros_like(bias_term)
        out_term[...] = jnp.zeros_like(out_term)

    across = (((1,), (1,)), ((), ()))
    down = (((0,), (0,)), ((), ()))
    grams = []
    xs = [x_ref[:, b].reshape(size, x_ref.shape[3]) for b in range(group)]
    for x in xs:
        gram = lax.dot_general(x, x, across, preferred_element_type=F32) * (1.0 / x.shape[1])
        grams.append(gram.astype(BF16))
    gram = jnp.concatenate(grams, axis=0)
    up = up_ref[...].reshape(group * size, up_ref.shape[2])
    pre = jnp.dot(gram, mix_ref[...], preferred_element_type=F32) + bias_ref[...]
    d_hidden = lax.dot_general(up, out_ref[...], across, preferred_element_type=F32)
    sig = jax.nn.sigmoid(pre)
    hidden = (pre * sig).astype(BF16)
    d_pre = (d_hidden * sig * (1.0 + pre * (1.0 - sig))).astype(BF16)
    comp = jnp.dot(hidden, out_ref[...], preferred_element_type=F32).astype(BF16)
    comp_ref[...] = comp.reshape(comp_ref.shape)
    out_term[...] += lax.dot_general(hidden, up, down, preferred_element_type=F32)
    mix_term[...] += lax.dot_general(gram, d_pre, down, preferred_element_type=F32)
    wide = d_pre.astype(F32)
    bias_term[...] += jnp.sum(wide.reshape(-1, 8, wide.shape[1]), axis=0)
    d_gram = lax.dot_general(d_pre, mix_ref[...], across, preferred_element_type=F32)
    for b in range(group):
        part = d_gram[b * size : (b + 1) * size]
        both = (part + part.T).astype(BF16)
        dx = jnp.dot(both, xs[b], preferred_element_type=F32) * (1.0 / x_ref.shape[3])
        dx_ref[:, b] = dx.astype(BF16).reshape(x_ref.shape[0], x_ref.shape[2], x_ref.shape[3])


def interact_rows(owned, upstream, mix_weight, mix_bias, out_weight, group=8):
    sources, count, parts, e = owned.shape
    f = sources * parts
    hidden, k = out_weight.shape
    rows = pl.BlockSpec((sources, group, parts, e), lambda i: (0, i, 0, 0))
    rows_k = pl.BlockSpec((group, f, k), lambda i: (i, 0, 0))

    def fixed(*shape):
        return pl.BlockSpec(shape, lambda i: (0,) * len(shape))

    return pl.pallas_call(
        interact_kernel,
        grid=(count // group,),
        in_specs=[rows, rows_k, fixed(f, hidden), fixed(1, hidden), fixed(hidden, k)],
        out_specs=[rows_k, rows, fixed(f, hidden), fixed(8, hidden), fixed(hidden, k)],
        out_shape=[
            jax.ShapeDtypeStruct((count, f, k), BF16),
            jax.ShapeDtypeStruct(owned.shape, BF16),
            jax.ShapeDtypeStruct((f, hidden), F32),
            jax.ShapeDtypeStruct((8, hidden), F32),
            jax.ShapeDtypeStruct((hidden, k), F32),
        ],
        cost_estimate=pl.CostEstimate(
            flops=2 * count * f * (2 * f * e + 6 * f * hidden),
            transcendentals=2 * count * f * hidden,
            bytes_accessed=8 * count * f * e,
        ),
        name="interact_rows",
    )(owned, upstream, mix_weight, mix_bias.reshape(1, -1), out_weight)


def step(value, pairs):
    return lax.ppermute(value, "tensor", pairs)


def swap(value):
    return lax.ppermute(value, "dp", [(0, 1), (1, 0)])


def place():
    index = lax.axis_index("tensor")
    z, y = index // 2, index % 2
    outer = (z == 0) | (z == 3)
    near = lax.axis_index("dp") == z // 2
    here, beside = z % 2, 1 - z % 2
    far_first = jnp.where(z < 2, 0, 1)
    first = jnp.where(near, here, far_first)
    second = jnp.where(near, beside, 1 - far_first)
    order = (2 * first + y, 2 * first + 1 - y, 2 * second + y, 2 * second + 1 - y)
    return outer, near, order


def after(value, *others):
    return lax.optimization_barrier((value, *others))[0]


def hold(values, *others):
    return lax.optimization_barrier((*values, *others))[: len(values)]


def add(a, b):
    return (a.astype(F32) + b.astype(F32)).astype(BF16)


def roles(pieces, q, near):
    own, other = pieces[q]
    other = swap(other)
    return jnp.where(near, own, other), jnp.where(near, other, own)


def interact(owned, cotangent, mix_weight, mix_bias, out_weight):
    count = owned.shape[1]
    comp, d_rows, mix_term, bias_term, out_term = interact_rows(
        owned, cotangent.reshape(count, F, K), mix_weight, mix_bias, out_weight
    )
    return comp.reshape(count, F * K), d_rows, mix_term, jnp.sum(bias_term, axis=0), out_term


def exchange_rows(value, owners):
    if value.ndim == 2:
        value = value.reshape(owners, value.shape[0] // owners, value.shape[1] // E, E)
        return lax.all_to_all(value, "tensor", split_axis=0, concat_axis=0, tiled=True)
    value = lax.all_to_all(value, "tensor", split_axis=0, concat_axis=0, tiled=True)
    return value.reshape(value.shape[0] * value.shape[1], value.shape[2] * value.shape[3])


def grid_sum_start(terms):
    mix_term, bias_term, out_term = (x + y for x, y in zip(*terms))
    mixed = jnp.concatenate([mix_term, jnp.broadcast_to(bias_term[None], (8, bias_term.shape[0]))], axis=0)
    wide = out_term.reshape(-1, mixed.shape[1])
    wide = jnp.concatenate([wide, jnp.zeros((mixed.shape[0] - wide.shape[0], wide.shape[1]), F32)], axis=0)
    first = lax.axis_index("dp") == 0
    return jnp.where(first, mixed, wide) + swap(jnp.where(first, wide, mixed).astype(BF16)).astype(F32)


def grid_sum_step(kept, pairs):
    sent = kept.astype(BF16)
    return sent.astype(F32) + step(sent, pairs).astype(F32)


def grid_sum_end(kept, out_shape):
    kept = kept.astype(BF16)
    other = swap(kept)
    first = lax.axis_index("dp") == 0
    mixed, wide = jnp.where(first, kept, other), jnp.where(first, other, kept)
    rows = out_shape[0] * out_shape[1] // kept.shape[1]
    return mixed[:-8].astype(F32), mixed[-8].astype(F32), wide[:rows].astype(F32).reshape(out_shape)


def grid_path(own, cross_w, cross_b, cotangent, small):
    outer, near, order = place()

    def four(close, distant):
        return close, distant, swap(close), swap(distant)

    def linear(pieces, *beside):
        total, other = hold(forward_rows(pieces, order, near, cross_w), *beside)
        return total + swap(other).astype(F32) + cross_b

    def back(d_linear, other, pair, *beside):
        outs = hold(back_part(d_linear, other, [order[q] for q in pair], cross_w), *beside)
        return {pair[0]: outs[:2], pair[1]: outs[2:]}

    def to_owner(c, line):
        base = own[c].astype(F32)
        return exchange_rows((base * line + base).astype(BF16), 8)

    def exchange(pieces, q):
        close, distant = roles(pieces, q, near)
        return distant, close

    def product(c, d_crossed):
        d_linear = (d_crossed.astype(F32) * own[c].astype(F32)).astype(BF16)
        return d_linear, swap(d_linear)

    def finish(c, d_crossed, line, back):
        return (d_crossed.astype(F32) * (line + 1.0) + back).astype(BF16)

    a, b = own
    y0, e1, m1 = step(a, ACROSS), step(a, PAIR), step(a, MID)
    y1, m2 = step(after(e1, y0, m1), ACROSS), step(after(e1, y0, m1), MID)
    e2 = step(after(m1, y0, e1), OUT)
    b2 = jnp.where(outer, e2, m1)
    y2, e3 = step(after(b2, y1, m2), ACROSS), step(after(m2, y1, e2), OUT)
    b3 = jnp.where(outer, e3, m2)
    y3 = step(after(b3, y2), ACROSS)
    first = after(b, y2, e3)
    f1, n1 = step(first, PAIR), step(first, MID)
    pieces = [four(a, b2), four(y0, y2), four(e1, b3), four(y1, y3)]
    x0 = step(after(b, y3, f1), ACROSS)
    x1, n2, f2 = step(after(f1, y3, n1), ACROSS), step(after(f1, y3, n1), MID), step(after(n1, y3, f1), OUT)
    line_a = linear(pieces, x0, x1, n2, f2)
    b2 = jnp.where(outer, f2, n1)
    x2, f3 = step(after(b2, x0, x1, n2), ACROSS), step(after(n2, x1, f2), OUT)
    owned_a = to_owner(0, after(line_a, b2))
    b3 = jnp.where(outer, f3, n2)
    x3 = step(after(b3, x2), ACROSS)
    out_a, d_rows_a, *terms_a = interact(after(owned_a, x2, f3), cotangent[0], *small)
    back_a = exchange_rows(d_rows_a, 8)
    pieces = [four(after(b, d_rows_a), b2), four(x0, x2), four(f1, b3), four(x1, x3)]
    line_b = linear(pieces, back_a)
    owned_b = to_owner(1, line_b)
    d_linear, other = product(0, back_a)
    part = back(after(d_linear, line_b), other, (3, 1), owned_b)
    distant3, close3 = exchange(part, 3)
    distant1, close1 = exchange(part, 1)
    g3, g1 = step(distant3, ACROSS), step(after(distant1, distant3), ACROSS)
    out_b, d_rows_b, *terms_b = interact(after(owned_b, distant3, distant1), cotangent[1], *small)
    back_b = exchange_rows(d_rows_b, 8)
    kept = grid_sum_start((terms_a, terms_b))
    second = back(after(d_linear, d_rows_b), other, (2, 0), g3, back_b)
    h3, h1 = step(after(close3, g3), ACROSS), step(after(close1, g3), ACROSS)
    distant2, close2 = exchange(second, 2)
    close0, distant0 = roles(second, 0, near)
    b3 = add(distant2, g3)
    b2 = add(after(distant0, b3), g1)
    k3, r2 = step(b3, INN), step(b2, INN)
    kept = grid_sum_step(after(kept, second[2][0]), PAIR)
    d_next, other = product(1, back_b)
    part = back(after(d_next, b3), other, (3, 1), k3, h3, kept)
    distant3, close3 = exchange(part, 3)
    distant1, close1 = exchange(part, 1)
    g3, g1 = step(after(distant3, h3), ACROSS), step(after(distant1, distant3), ACROSS)
    k3, kept = hold((k3, kept), distant3, distant1)
    b3, e1 = add(b3, k3), add(close2, h3)
    k2 = step(b3, MID)
    sent = kept.astype(BF16)
    got = step(sent, CROSS)
    sum_a = close0.astype(F32) + h1.astype(F32)
    second = back(after(d_next, distant3, distant1), other, (2, 0), h1, r2, k2)
    h3, h1 = step(after(close3, g3), ACROSS), step(after(close1, g3), ACROSS)
    distant2, close2 = exchange(second, 2)
    close0, distant0 = roles(second, 0, near)
    b3 = add(distant2, g3)
    k3 = step(b3, INN)
    k2, r2, got = hold((k2, r2, got), b3)
    sent = (sent.astype(F32) + got.astype(F32)).astype(BF16)
    got = step(sent, ACROSS)
    r0_a = step(add(b2, r2), MID)
    e1 = add(e1, k2)
    b2 = add(after(distant0, b3), g1)
    r2 = step(b2, INN)
    b3 = add(b3, k3)
    k2 = step(b3, MID)
    r1_a = step(after(e1, b2), PAIR)
    e1 = add(add(close2, h3), k2)
    r1 = step(e1, PAIR)
    r0 = step(add(b2, r2), MID)
    r0_a, r1_a, got = hold((r0_a, r1_a, got), r2, k2)
    kept = sent.astype(F32) + got.astype(F32)
    sum_a = sum_a + r0_a.astype(F32) + r1_a.astype(F32)
    sums = grid_sum_end(kept, terms_a[2].shape)
    sum_b = close0.astype(F32) + h1.astype(F32) + r0.astype(F32) + r1.astype(F32)
    grad_a = finish(0, back_a, line_a, sum_a)
    grad_b = finish(1, back_b, line_b, sum_b)
    return (out_a, out_b), sums, (grad_a, grad_b)


def linear_any(own, cross_w, cross_b):
    rows = own.shape[0]
    full = lax.all_gather(own, "tensor", axis=1, tiled=True)
    half = full.shape[1] // 2
    core = lax.axis_index("dp")
    kept = lax.dynamic_slice_in_dim(full, core * half, half, 1)
    other = swap(lax.dynamic_slice_in_dim(full, (1 - core) * half, half, 1))
    total = jnp.dot(jnp.concatenate([kept, other], axis=0), cross_w, preferred_element_type=F32)
    return total[:rows] + swap(total[rows:].astype(BF16)).astype(F32) + cross_b


def back_any(d_linear, cross_w):
    rows = d_linear.shape[0]
    both = jnp.concatenate([d_linear, swap(d_linear)], axis=0)
    contract = (((1,), (1,)), ((), ()))
    terms = lax.dot_general(both, cross_w, contract, preferred_element_type=F32).astype(BF16)
    own, other = terms[:rows], swap(terms[rows:])
    first = lax.axis_index("dp") == 0
    full = jnp.concatenate([jnp.where(first, own, other), jnp.where(first, other, own)], axis=1)
    return lax.psum_scatter(full, "tensor", scatter_dimension=1, tiled=True).astype(F32)


def shards(inputs, cross_w, cross_b, mix_weight, mix_bias, out_weight, cotangent):
    own = inputs[0]
    rows, width = own.shape
    tensor_count, dp_count = lax.axis_size("tensor"), lax.axis_size("dp")
    small = mix_weight, mix_bias, out_weight
    if tensor_count == 8:
        half = rows // tensor_count // 2
        by_owner = own.reshape(tensor_count, 2 * half, width)
        halves = [by_owner[:, c * half : (c + 1) * half].reshape(rows // 2, width) for c in range(2)]
        up = [cotangent[0, c * half : (c + 1) * half] for c in range(2)]
        compressed, sums, grads = grid_path(halves, cross_w, cross_b, up, small)
        compressed = jnp.concatenate(compressed, axis=0)
        grads = [grad.reshape(tensor_count, half, width) for grad in grads]
        grad = jnp.concatenate(grads, axis=1).reshape(rows, width)
    else:
        base = own.astype(F32)
        linear = linear_any(own, cross_w, cross_b)
        owned = exchange_rows((base * linear + base).astype(BF16), tensor_count)
        compressed, d_rows, *terms = interact(owned, cotangent[0], *small)
        d_crossed = exchange_rows(d_rows, tensor_count).astype(F32)
        back = back_any((d_crossed * base).astype(BF16), cross_w)
        grad = (d_crossed * (linear + 1.0) + back).astype(BF16)
        sums = [value.astype(F32) for value in lax.psum([t.astype(BF16) for t in terms], ("tensor", "dp"))]
    row_total = rows * dp_count
    return compressed[None], grad[None], *(value / row_total for value in sums)


def solution(mesh):
    return jax.shard_map(
        shards,
        mesh=mesh,
        in_specs=(
            P(("groups", "dp"), None, "tensor"),
            P("dp", "tensor"),
            P("tensor"),
            P(),
            P(),
            P(),
            P(("groups", "dp"), "tensor", None),
        ),
        out_specs=(
            P(("groups", "dp"), "tensor", None),
            P(("groups", "dp"), None, "tensor"),
            P("groups", None),
            P("groups"),
            P("groups", None),
        ),
        check_vma=False,
    )
```
